512 devices in a mesh: tok: 16 (over z, y_hi), hid: 32 (over y_lo, x, core).
Axes of the slice: x: 4, y: 8 (y_hi: 2, y_lo: 4; y = y_hi * 4 + y_lo), z: 8, core: 2. Of those that a mesh axis runs over, the one named last changes fastest.
Arguments:
- resid_in: bfloat16 [512, 8192], P('hid', 'tok'), may hold values from -64 to 64
- norm_gain: float32 [8192], P('tok'), may hold values from 0.1 to 1.9
- gate_weight: bfloat16 [8192, 28672], P('tok', 'hid'), may hold values from -0.0625 to 0.0625
- up_weight: bfloat16 [8192, 28672], P('tok', 'hid'), may hold values from -0.0625 to 0.0625
- down_weight: bfloat16 [28672, 8192], P('hid', 'tok'), may hold values from -0.0625 to 0.0625
- labels: int32 [512], replicated, may hold values from 0 to 63
Outputs:
- gram: float32 [8192, 8192], P(('tok', 'hid'))
- cross: float32 [8192, 64], P(('tok', 'hid'))
The draws below stay inside these ranges and needn't reach their ends.
All inputs are finite; a program needn't handle non-finite values.
Results may differ from the reference program's by a relative error of at most 0.014.
Values may be sent and summed in bfloat16 or wider, within the bound.
A program may use at most 64 MiB of HBM per device.

```python
import math
import jax
import jax.numpy as jnp
from jax import lax

D = 8192
FF = 28672
CLASSES = 64
TOKENS = 512
N_TOK = 16


def draw_resid_in(key, part):
    keys = jax.random.split(key, 3)
    rowscale = jnp.exp(jax.random.uniform(keys[0], (TOKENS, 1), jnp.float32, math.log(0.3), math.log(3.0)))
    colrand = jnp.exp(jax.random.uniform(keys[1], (1, D), jnp.float32, math.log(0.5), math.log(2.0)))
    ramp = jnp.exp(math.log(3.0) * (jnp.arange(D, dtype=jnp.float32)[None, :] / float(D) - 0.5))
    colscale = colrand * ramp
    base = jax.random.normal(keys[2], (TOKENS, D), jnp.float32)
    values = jnp.clip(rowscale * colscale * base, -64.0, 64.0)
    return values.astype(jnp.bfloat16)


def draw_labels(key, part):
    keys = jax.random.split(jax.random.fold_in(key, 7), 4)
    middle = (1 + jax.random.permutation(keys[0], CLASSES - 2)).astype(jnp.int32)
    allowed = jnp.concatenate([jnp.array([0, CLASSES - 1], jnp.int32), middle[:CLASSES - 4]])
    first = jax.random.randint(keys[1], (TOKENS,), 0, CLASSES - 2)
    second = jax.random.randint(keys[2], (TOKENS,), 0, CLASSES - 2)
    labels = allowed[jnp.minimum(first, second)]
    places = jax.random.permutation(keys[3], TOKENS)
    labels = labels.at[places[0]].set(0).at[places[1]].set(CLASSES - 1)
    return labels.astype(jnp.int32)


def with_spikes(values, key, source, target, shards_of, factor):
    def block_of(axis_at):
        return (jnp.arange(values.shape[axis_at]) // (values.shape[axis_at] // shards_of)).reshape((-1,) + (1,) * (values.ndim - 1 - axis_at))

    first = jax.random.permutation(key, shards_of)[block_of(target)]
    other_side = (block_of(target) + shards_of // 2) % shards_of
    return jnp.where((block_of(source) == first) | (block_of(source) == other_side), factor * values, values)


def shard_levels(stream_key, dims, pieces, smallest, top_value):
    gain, own = 1.0, jax.random.fold_in(stream_key, 6)
    for dim, parts in pieces:
        draws = jnp.exp(jax.random.uniform(jax.random.fold_in(own, dim), (parts,), jnp.float32, smallest / len(pieces), top_value / len(pieces)))
        gain = gain * jnp.repeat(draws, dims[dim] // parts).reshape([-1 if axis == dim else 1 for axis in range(len(dims))])
    return gain


def centred(key, dims, scale, limit, pieces=(), held_as=jnp.bfloat16):
    drawn = scale * jax.random.normal(key, dims, jnp.float32)
    if pieces:
        drawn = drawn * shard_levels(key, dims, pieces, -0.22, 0.18)
    return jnp.clip(drawn, -limit, limit).astype(held_as)


def gaussian_with(own_key, extent, scale, most, pieces, heavy, kind=jnp.bfloat16):
    drawn = scale * jax.random.normal(own_key, extent, jnp.float32)
    if pieces:
        drawn = drawn * shard_levels(own_key, extent, pieces, -0.22, 0.18)
    return jnp.clip(with_spikes(drawn, jax.random.fold_in(own_key, 3), *heavy), -most, most).astype(kind)


def setup_inputs(seed: int = 0) -> dict:
    arg_keys = jax.random.split(jax.random.key(seed), 7)
    resid_in = draw_resid_in(jax.random.fold_in(arg_keys[6], 71), 0)
    norm_gain = jnp.clip(1.0 + 0.18 * jax.random.normal(arg_keys[1], (D,), jnp.float32), 0.1, 1.9)
    gate_weight = centred(arg_keys[2], (D, FF), D ** -0.5, 0.0625, ((0, 16), (1, 32)))
    up_weight = centred(arg_keys[3], (D, FF), D ** -0.5, 0.0625, ((0, 16), (1, 32)))
    down_weight = gaussian_with(arg_keys[4], (FF, D), FF ** -0.5, 0.0625, ((0, 32), (1, 16)), (0, 1, 32, 2.75))
    labels = draw_labels(jax.random.fold_in(arg_keys[6], 71), 0)
    return {"resid_in": resid_in, "norm_gain": norm_gain, "gate_weight": gate_weight, "up_weight": up_weight, "down_weight": down_weight, "labels": labels}


def reference(resid_in, norm_gain, gate_weight, up_weight, down_weight, labels):
    xf = resid_in.astype(jnp.float32)
    meansq = lax.optimization_barrier(jnp.mean(xf * xf, axis=1, keepdims=True))
    normed = (xf * lax.rsqrt(meansq + 1e-05) * norm_gain[None, :]).astype(jnp.bfloat16)
    width = D // N_TOK
    gate = jnp.zeros((resid_in.shape[0], FF), jnp.float32)
    up = jnp.zeros((resid_in.shape[0], FF), jnp.float32)
    for block in range(N_TOK):
        rows = normed[:, block * width:(block + 1) * width]
        term_g = lax.optimization_barrier(jnp.dot(rows, gate_weight[block * width:(block + 1) * width], preferred_element_type=jnp.float32).astype(jnp.bfloat16))
        term_u = lax.optimization_barrier(jnp.dot(rows, up_weight[block * width:(block + 1) * width], preferred_element_type=jnp.float32).astype(jnp.bfloat16))
        gate = gate + term_g.astype(jnp.float32)
        up = up + term_u.astype(jnp.float32)
    hidden = (jax.nn.silu(gate) * up).astype(jnp.bfloat16)
    mlp_out = jnp.dot(hidden, down_weight, preferred_element_type=jnp.float32)
    resid = (xf + mlp_out).astype(jnp.bfloat16)
    gram = jnp.dot(resid.T, resid, preferred_element_type=jnp.float32) / float(resid.shape[0])
    onehot = (labels[:, None] == jnp.arange(CLASSES, dtype=jnp.int32)[None, :]).astype(jnp.bfloat16)
    counts = lax.optimization_barrier(jnp.sum(onehot.astype(jnp.float32), axis=0))
    cross = jnp.dot(resid.T, onehot, preferred_element_type=jnp.float32) / jnp.maximum(counts, 1.0)[None, :]
    return (gram, cross)
```

```python
import jax
import jax.numpy as jnp
from jax import lax
from jax.experimental import pallas as pl
from jax.experimental.pallas import tpu as pltpu
from jax.sharding import PartitionSpec as P

CLASSES = 64
EPS = 1e-05
F32 = jnp.float32
BF16 = jnp.bfloat16
MESH = pl.DeviceIdType.MESH
NT = (((1,), (1,)), ((), ()))


def kernel(x_ref, gain_ref, wg_hbm, wu_hbm, wd_hbm, lab_ref, gram_ref, cross_ref,
           xg, xn, wg, wu, wd, wdt, sqb, sqz, sqp, cown, csend, crecv, fin, ysend, yrecv,
           hb, ot, es, er, ea, ex, exr, ey, eyr, cb, rb, gt, gr,
           wsem, a_s, a_r, q_s, q_r, c_s, c_r, y_s, y_r, d_s, d_r, e_s, e_r, f_s, f_r):
    t = lax.axis_index("tok")
    h = lax.axis_index("hid")
    z, yh = t // 2, lax.rem(t, 2)
    yl, x, c = h // 8, lax.rem(h // 2, 4), lax.rem(h, 2)
    y = yh * 4 + yl

    def at(z=z, y=y, x=x, c=c):
        return {"tok": z * 2 + y // 4, "hid": (lax.rem(y, 4) * 4 + x) * 2 + c}

    def zp(d):
        return at(z=lax.rem(z + d + 8, 8))

    def yp(d):
        return at(y=lax.rem(y + d + 8, 8))

    def ylp(d):
        return at(y=yh * 4 + lax.rem(yl + d, 4))

    def xp(d):
        return at(x=lax.rem(x + d, 4))

    sib = at(c=1 - c)
    part = yp(4)

    loads = [pltpu.make_async_copy(a, b, wsem.at[i])
             for i, (a, b) in enumerate(((wg_hbm, wg), (wu_hbm, wu), (wd_hbm, wd)))]
    for cp in loads:
        cp.start()

    barrier = pltpu.get_barrier_semaphore()
    peers = [zp(d) for d in range(1, 8)] + [yp(d) for d in range(1, 8)]
    peers += [xp(d) for d in range(1, 4)] + [sib]
    for p in peers:
        pl.semaphore_signal(barrier, inc=1, device_id=p, device_id_type=MESH)
    xg[yl, x, c] = x_ref[...]
    pl.semaphore_wait(barrier, len(peers))

    sends = []

    def rcopy(src, dst, ss, rs, dev):
        cp = pltpu.make_async_remote_copy(src_ref=src, dst_ref=dst, send_sem=ss, recv_sem=rs,
                                          device_id=dev, device_id_type=MESH)
        cp.start()
        return cp

    def put(src, dst, ss, rs, dev):
        cp = rcopy(src, dst, ss, rs, dev)
        sends.append(cp)
        return cp

    cps = [put(xg.at[yl, x, c], xg.at[yl, x, c], a_s.at[d - 1], a_r.at[d - 1], ylp(d)) for d in (1, 2, 3)]
    for cp in cps:
        cp.wait_recv()
    cps = [put(xg.at[:, x, c], xg.at[:, x, c], a_s.at[d + 2], a_r.at[d + 2], xp(d)) for d in (1, 2, 3)]
    for cp in cps:
        cp.wait_recv()
    cp = put(xg.at[:, :, c], xg.at[:, :, c], a_s.at[6], a_r.at[6], sib)
    cp.wait_recv()

    xa = xg[...].reshape(512, 512)
    xf = xa.astype(F32)
    xn[...] = (xf * gain_ref[...]).astype(BF16)
    for cp in loads:
        cp.wait()

    def own(q, sub):
        rows = xn[pl.ds(pl.multiple_of(q * 64 + sub * 32, 32), 32), :]
        cown[sub, 0] = jnp.dot(rows, wg[...], preferred_element_type=F32)
        cown[sub, 1] = jnp.dot(rows, wu[...], preferred_element_type=F32)

    right, left = zp(1), zp(-1)
    streams = [(0, 0), (1, 0), (0, 1), (1, 1)]

    def ring(k, s):
        sub, half = s
        return pltpu.make_async_remote_copy(
            src_ref=csend.at[k, sub, half], dst_ref=crecv.at[k, sub, half],
            send_sem=c_s.at[k, sub, half], recv_sem=c_r.at[k, sub, half],
            device_id=right if sub == 0 else left, device_id_type=MESH)

    def owns(k):
        own(lax.rem(z + 15 - k, 8), 0)
        own(lax.rem(z + 1 + k, 8), 1)

    owns(0)
    for s in streams:
        csend[0, s[0], s[1]] = cown[s[0], s[1]].astype(BF16)
        ring(0, s).start()

    x2 = xf * xf
    hi = x2.astype(BF16)
    lo = (x2 - hi.astype(F32)).astype(BF16)
    ones = jnp.ones((8, 512), BF16)
    sq = (lax.dot_general(ones, hi, NT, preferred_element_type=F32)
          + lax.dot_general(ones, lo, NT, preferred_element_type=F32))
    sqb[...] = jnp.zeros_like(sqb)
    for k in range(4):
        sqb[k:k + 1, :] = sq[0:1, k * 128:(k + 1) * 128]
    qcps = [put(sqb, sqz.at[d - 1], q_s.at[d - 1], q_r.at[d - 1], zp(d)) for d in range(1, 8)]

    def step(k, _):
        owns(k)
        for s in streams:
            ring(k - 1, s).wait_recv()
            csend[k, s[0], s[1]] = (cown[s[0], s[1]] + crecv[k - 1, s[0], s[1]].astype(F32)).astype(BF16)
            ring(k, s).start()
        return 0

    lax.fori_loop(1, 7, step, 0)

    own(z, 0)
    own(z, 1)
    for cp in qcps:
        cp.wait_recv()
    tot = sqb[...]
    for d in range(7):
        tot = tot + sqz[d]
    sqp[0] = tot
    qy = put(sqp.at[0], sqp.at[1], q_s.at[7], q_r.at[7], part)
    wdt[...] = wd[...].T
    sel = (lax.broadcasted_iota(jnp.int32, (16, 512), 1)
           == lax.broadcasted_iota(jnp.int32, (16, 512), 0) + h * 16).astype(BF16)
    xcols = lax.dot_general(sel, xa, NT, preferred_element_type=F32)
    onehot = (lax.broadcasted_iota(jnp.int32, (CLASSES, 512), 0) == lab_ref[...]).astype(BF16)
    counts = lax.dot_general(ones, onehot, NT, preferred_element_type=F32)
    qy.wait_recv()
    tot = sqp[0] + sqp[1]
    tix = (lax.broadcasted_iota(jnp.int32, (64, 128), 0) + z * 64
           - lax.broadcasted_iota(jnp.int32, (64, 128), 1))
    pick = jnp.zeros((64, 128), F32)
    for k in range(4):
        pick = pick + jnp.where(tix == k * 128, tot[k:k + 1, :], 0.0)
    scale = lax.rsqrt(jnp.sum(pick, axis=1, keepdims=True) / 8192.0 + EPS)

    ycps = []
    for s in streams:
        sub, half = s
        ring(6, s).wait_recv()
        v = cown[sub, half] + crecv[6, sub, half].astype(F32)
        fin[sub, half] = v
        ysend[sub, half] = v.astype(BF16)
        ycps.append(put(ysend.at[sub, half], yrecv.at[sub, half], y_s.at[sub, half], y_r.at[sub, half], part))
    for cp in ycps:
        cp.wait_recv()
    for sub in range(2):
        sc = scale[sub * 32:(sub + 1) * 32, :]
        gate = (fin[sub, 0] + yrecv[sub, 0].astype(F32)) * sc
        up = (fin[sub, 1] + yrecv[sub, 1].astype(F32)) * sc
        hb[z, sub] = (gate / (1.0 + jnp.exp(-gate)) * up).astype(BF16)

    def dput(k, way, sub):
        q = lax.rem(z + 8 - k, 8) if way == 0 else lax.rem(z + k, 8)
        return put(hb.at[q, sub], hb.at[q, sub], d_s.at[k, way, sub], d_r.at[k, way, sub],
                   right if way == 0 else left)

    live = {}
    for sub in range(2):
        for way in range(2):
            live[way, sub] = dput(0, way, sub)
    for k in range(1, 4):
        for sub in range(2):
            for way in range(2):
                live[way, sub].wait_recv()
                if k < 3 or way == sub:
                    live[way, sub] = dput(k, way, sub)
    live[0, 0].wait_recv()
    live[1, 1].wait_recv()

    hall = hb[...].reshape(512, 896)
    ot[...] = lax.dot_general(wdt[...], hall, NT, preferred_element_type=F32).reshape(4, 4, 2, 16, 512)

    es[...] = ot[:, :, 1 - c].astype(BF16)
    cp = put(es, er, e_s.at[0], e_r.at[0], sib)
    cp.wait_recv()
    v = ot[:, :, c] + er[...].astype(F32)
    ea[...] = v
    ex[...] = v.astype(BF16)
    cps = [put(ex.at[:, lax.rem(x + d, 4)], exr.at[d - 1], e_s.at[d], e_r.at[d], xp(d)) for d in (1, 2, 3)]
    for cp in cps:
        cp.wait_recv()
    v = ea[:, x]
    for d in range(3):
        v = v + exr[d].astype(F32)
    ea[:, 0] = v
    ey[...] = v.astype(BF16)
    cps = [put(ey.at[lax.rem(yl + d, 4)], eyr.at[d - 1], e_s.at[d + 3], e_r.at[d + 3], ylp(d)) for d in (1, 2, 3)]
    for cp in cps:
        cp.wait_recv()
    m = ea[yl, 0]
    for d in range(3):
        m = m + eyr[d].astype(F32)
    r = (xcols + m).astype(BF16)

    cb[z, x, c] = r
    rb[y] = r
    zc = [put(cb.at[z, x, c], cb.at[z, x, c], f_s.at[d - 1], f_r.at[d - 1], zp(d)) for d in range(1, 8)]
    yc = [put(cb.at[z, x, c], rb.at[y], f_s.at[d + 6], f_r.at[d + 6], yp(d)) for d in range(1, 8)]
    csum = lax.dot_general(r, onehot, NT, preferred_element_type=F32)
    cross_ref[...] = csum / jnp.maximum(counts[0:1, :], 1.0)
    for cp in zc:
        cp.wait_recv()
    cps = [put(cb.at[:, x, c], cb.at[:, x, c], f_s.at[d + 13], f_r.at[d + 13], xp(d)) for d in (1, 2, 3)]
    for cp in cps:
        cp.wait_recv()
    cp = put(cb.at[:, :, c], cb.at[:, :, c], f_s.at[17], f_r.at[17], sib)
    for q in yc:
        q.wait_recv()
    cp.wait_recv()
    rows = rb[...].reshape(128, 512)
    for zz in range(8):
        g = lax.dot_general(rows, cb[zz].reshape(128, 512), NT, preferred_element_type=F32)
        gt[:, :, zz * 128:(zz + 1) * 128] = (g * (1.0 / 512.0)).astype(BF16).reshape(8, 16, 128)
    cps = [put(gt.at[lax.rem(y + d, 8)], gr.at[y], f_s.at[d + 17], f_r.at[d + 17], yp(d)) for d in range(1, 8)]
    gr[y] = gt[y]
    for cp in cps:
        cp.wait_recv()
    for yy in range(8):
        for zz in range(8):
            o = (zz * 2 + yy // 4) * 512 + (yy % 4) * 128
            gram_ref[:, o:o + 128] = gr[yy, :, zz * 128:(zz + 1) * 128].astype(F32)

    for cp in sends:
        cp.wait_send()

    def drain(k, _):
        for s in streams:
            ring(k, s).wait_send()
        return 0

    lax.fori_loop(0, 7, drain, 0)


def on_device(resid_in, norm_gain, gate_weight, up_weight, down_weight, labels):
    vm = pl.BlockSpec(memory_space=pltpu.VMEM)
    hbm = pl.BlockSpec(memory_space=pltpu.HBM)
    dma = pltpu.SemaphoreType.DMA
    scratch = [
        pltpu.VMEM((4, 4, 2, 16, 512), BF16),
        pltpu.VMEM((512, 512), BF16),
        pltpu.VMEM((512, 896), BF16),
        pltpu.VMEM((512, 896), BF16),
        pltpu.VMEM((896, 512), BF16),
        pltpu.VMEM((512, 896), BF16),
        pltpu.VMEM((8, 128), F32),
        pltpu.VMEM((7, 8, 128), F32),
        pltpu.VMEM((2, 8, 128), F32),
        pltpu.VMEM((2, 2, 32, 896), F32),
        pltpu.VMEM((7, 2, 2, 32, 896), BF16),
        pltpu.VMEM((7, 2, 2, 32, 896), BF16),
        pltpu.VMEM((2, 2, 32, 896), F32),
        pltpu.VMEM((2, 2, 32, 896), BF16),
        pltpu.VMEM((2, 2, 32, 896), BF16),
        pltpu.VMEM((8, 2, 32, 896), BF16),
        pltpu.VMEM((4, 4, 2, 16, 512), F32),
        pltpu.VMEM((4, 4, 16, 512), BF16),
        pltpu.VMEM((4, 4, 16, 512), BF16),
        pltpu.VMEM((4, 4, 16, 512), F32),
        pltpu.VMEM((4, 4, 16, 512), BF16),
        pltpu.VMEM((3, 4, 16, 512), BF16),
        pltpu.VMEM((4, 16, 512), BF16),
        pltpu.VMEM((3, 16, 512), BF16),
        pltpu.VMEM((8, 4, 2, 16, 512), BF16),
        pltpu.VMEM((8, 16, 512), BF16),
        pltpu.VMEM((8, 16, 1024), BF16),
        pltpu.VMEM((8, 16, 1024), BF16),
        dma((3,)),
        dma((7,)), dma((7,)),
        dma((8,)), dma((8,)),
        dma((7, 2, 2)), dma((7, 2, 2)),
        dma((2, 2)), dma((2, 2)),
        dma((4, 2, 2)), dma((4, 2, 2)),
        dma((7,)), dma((7,)),
        dma((25,)), dma((25,)),
    ]
    return pl.pallas_call(
        kernel,
        out_shape=(jax.ShapeDtypeStruct((16, 8192), F32), jax.ShapeDtypeStruct((16, CLASSES), F32)),
        in_specs=[vm, vm, hbm, hbm, hbm, vm],
        out_specs=(vm, vm),
        scratch_shapes=scratch,
        compiler_params=pltpu.CompilerParams(
            collective_id=0, has_side_effects=True, vmem_limit_bytes=60 * 2**20),
    )(resid_in, norm_gain.reshape(1, -1), gate_weight, up_weight, down_weight, labels.reshape(1, -1))


def solution(mesh):
    return jax.shard_map(
        on_device,
        mesh=mesh,
        in_specs=(P("hid", "tok"), P("tok"), P("tok", "hid"), P("tok", "hid"), P("hid", "tok"), P()),
        out_specs=(P(("tok", "hid"), None), P(("tok", "hid"), None)),
        check_vma=False,
    )
```

```python
import jax
import jax.numpy as jnp
from jax import lax
from jax.experimental import pallas as pl
from jax.experimental.pallas import tpu as pltpu
from jax.sharding import PartitionSpec as P

CLASSES = 64
EPS = 1e-05
F32 = jnp.float32
BF16 = jnp.bfloat16
MESH = pl.DeviceIdType.MESH
NT = (((1,), (1,)), ((), ()))


def kernel(x_ref, gain_ref, wg_hbm, wu_hbm, wd_hbm, lab_ref, gram_ref, cross_ref,
           xg, xn, wg, wu, wd, wdt, sqb, sqz, sqp, cown, csend, crecv, fin, ysend, yrecv,
           hb, ot, es, er, ea, ex, exr, ey, eyr, cb, rb, gt, gr,
           wsem, a_s, a_r, q_s, q_r, c_s, c_r, y_s, y_r, d_s, d_r, e_s, e_r, f_s, f_r):
    t = lax.axis_index("tok")
    h = lax.axis_index("hid")
    z, yh = t // 2, lax.rem(t, 2)
    yl, x, c = h // 8, lax.rem(h // 2, 4), lax.rem(h, 2)
    y = yh * 4 + yl

    def at(z=z, y=y, x=x, c=c):
        return {"tok": z * 2 + y // 4, "hid": (lax.rem(y, 4) * 4 + x) * 2 + c}

    def zp(d):
        return at(z=lax.rem(z + d, 8))

    def yp(d):
        return at(y=lax.rem(y + d, 8))

    def ylp(d):
        return at(y=yh * 4 + lax.rem(yl + d, 4))

    def xp(d):
        return at(x=lax.rem(x + d, 4))

    sib = at(c=1 - c)
    part = yp(4)

    loads = [pltpu.make_async_copy(a, b, wsem.at[i])
             for i, (a, b) in enumerate(((wg_hbm, wg), (wu_hbm, wu), (wd_hbm, wd)))]
    for cp in loads:
        cp.start()

    barrier = pltpu.get_barrier_semaphore()
    peers = [zp(d) for d in range(1, 8)] + [yp(d) for d in range(1, 8)]
    peers += [xp(d) for d in range(1, 4)] + [sib]
    for p in peers:
        pl.semaphore_signal(barrier, inc=1, device_id=p, device_id_type=MESH)
    xg[yl, x, c] = x_ref[...]
    pl.semaphore_wait(barrier, len(peers))

    sends = []

    def put(src, dst, sem, i, dev):
        cp = pltpu.make_async_remote_copy(src_ref=src, dst_ref=dst, send_sem=sem[0].at[i], recv_sem=sem[1].at[i],
                                          device_id=dev, device_id_type=MESH)
        cp.start()
        sends.append(cp)
        return cp

    sa = (a_s, a_r)
    ycp = [put(xg.at[yl, x, c], xg.at[yl, x, c], sa, d - 1, ylp(d)) for d in (1, 2, 3)]
    xcp = [[put(xg.at[yl, x, c], xg.at[yl, x, c], sa, d + 2, xp(d)) for d in (1, 2, 3)]]
    loads[2].wait()
    wdt[...] = wd[...].T
    for d in (1, 2, 3):
        ycp[d - 1].wait_recv()
        b = lax.rem(yl + 4 - d, 4)
        xcp.append([put(xg.at[b, x, c], xg.at[b, x, c], sa, 3 * d + e + 2, xp(e)) for e in (1, 2, 3)])
    scp = []
    for d in range(4):
        for cp in xcp[d]:
            cp.wait_recv()
        b = lax.rem(yl + 4 - d, 4)
        scp.append(put(xg.at[b, :, c], xg.at[b, :, c], sa, 15 + d, sib))
    loads[0].wait()
    loads[1].wait()
    for cp in scp:
        cp.wait_recv()

    xa = xg[...].reshape(512, 512)
    xf = xa.astype(F32)
    xn[...] = (xf * gain_ref[...]).astype(BF16)

    def own(r):
        q = lax.rem(z + r, 8)
        rows = xn[pl.ds(pl.multiple_of(q * 64, 64), 64), :]
        cown[r, :, :, :896] = jnp.dot(rows, wg[...], preferred_element_type=F32).reshape(4, 16, 896)
        cown[r, :, :, 896:] = jnp.dot(rows, wu[...], preferred_element_type=F32).reshape(4, 16, 896)

    right, left = zp(1), zp(7)
    sc = (c_s, c_r)
    ring = {}

    def hop(k, way, s, add):
        r = 4 - k if way == 0 else 4 + k
        v = cown[r, s]
        if add:
            ring[k - 1, way, s].wait_recv()
            v = v + crecv[k - 1, way, s].astype(F32)
        csend[k, way, s] = v.astype(BF16)
        ring[k, way, s] = put(csend.at[k, way, s], crecv.at[k, way, s], sc, (k, way, s), right if way == 0 else left)

    own(4)
    for i in (0, 1):
        hop(0, 0, i, False)
        hop(0, 1, 2 + i, False)
    own(3)
    own(5)
    for i in (0, 1):
        hop(1, 0, 2 + i, False)
        hop(1, 1, i, False)

    x2 = xf * xf
    hi = x2.astype(BF16)
    lo = (x2 - hi.astype(F32)).astype(BF16)
    ones = jnp.ones((8, 512), BF16)
    sq = (lax.dot_general(ones, hi, NT, preferred_element_type=F32)
          + lax.dot_general(ones, lo, NT, preferred_element_type=F32))
    sqb[...] = jnp.zeros_like(sqb)
    for k in range(4):
        sqb[k:k + 1, :] = sq[0:1, k * 128:(k + 1) * 128]
    sqs = (q_s, q_r)
    qcps = [put(sqb, sqz.at[d - 1], sqs, d - 1, zp(d)) for d in range(1, 8)]

    for i in (0, 1):
        hop(1, 0, i, True)
        hop(1, 1, 2 + i, True)
    order = [(0, 2), (1, 0), (0, 3), (1, 1), (0, 0), (1, 2), (0, 1), (1, 3)]
    own(2)
    own(6)
    for way, s in order:
        hop(2, way, s, True)
    own(1)
    own(7)
    for way, s in order:
        hop(3, way, s, True)
    own(0)

    for cp in qcps:
        cp.wait_recv()
    tot = sqb[...]
    for d in range(7):
        tot = tot + sqz[d]
    sqp[0] = tot
    qy = put(sqp.at[0], sqp.at[1], sqs, 7, part)
    sel = (lax.broadcasted_iota(jnp.int32, (16, 512), 1)
           == lax.broadcasted_iota(jnp.int32, (16, 512), 0) + h * 16).astype(BF16)
    xcols = lax.dot_general(sel, xa, NT, preferred_element_type=F32)
    onehot = (lax.broadcasted_iota(jnp.int32, (CLASSES, 512), 0) == lab_ref[...]).astype(BF16)
    counts = lax.dot_general(ones, onehot, NT, preferred_element_type=F32)

    srow = (2, 0, 3, 1)
    sy = (y_s, y_r)
    ycps = {}
    for s in srow:
        ring[3, 0, s].wait_recv()
        ring[3, 1, s].wait_recv()
        v = cown[0, s] + crecv[3, 0, s].astype(F32) + crecv[3, 1, s].astype(F32)
        fin[s] = v
        ysend[s] = v.astype(BF16)
        ycps[s] = put(ysend.at[s], yrecv.at[s], sy, s, part)
    qy.wait_recv()
    tot = sqp[0] + sqp[1]
    tix = (lax.broadcasted_iota(jnp.int32, (64, 128), 0) + z * 64
           - lax.broadcasted_iota(jnp.int32, (64, 128), 1))
    pick = jnp.zeros((64, 128), F32)
    for k in range(4):
        pick = pick + jnp.where(tix == k * 128, tot[k:k + 1, :], 0.0)
    scale = lax.rsqrt(jnp.sum(pick, axis=1, keepdims=True) / 8192.0 + EPS)

    sd = (d_s, d_r)

    def dput(k, way, s):
        q = lax.rem(z + 8 - k, 8) if way == 0 else lax.rem(z + k, 8)
        return put(hb.at[q, s], hb.at[q, s], sd, (k, way, s), right if way == 0 else left)

    live = {}
    for s in srow:
        ycps[s].wait_recv()
        v = (fin[s] + yrecv[s].astype(F32)) * scale[s * 16:(s + 1) * 16, :]
        gate, up = v[:, :896], v[:, 896:]
        hb[z, s] = (gate / (1.0 + jnp.exp(-gate)) * up).astype(BF16)
        for way in (0, 1):
            live[0, way, s] = dput(0, way, s)
    for k in (1, 2, 3):
        for s in srow:
            for way in (0, 1):
                live[k - 1, way, s].wait_recv()
                if k < 3 or way == s // 2:
                    live[k, way, s] = dput(k, way, s)
    for s in srow:
        live[3, s // 2, s].wait_recv()

    se = (e_s, e_r)
    hall = hb[...].reshape(512, 896)
    eo = (2, 1, 3, 0)
    scp = {}
    for d in eo:
        b = lax.rem(yl + d, 4)
        w = wdt[pl.ds(pl.multiple_of(b * 128, 128), 128), :]
        ot[d] = lax.dot_general(w, hall, NT, preferred_element_type=F32).reshape(4, 2, 16, 512)
        es[d] = ot[d, :, 1 - c].astype(BF16)
        scp[d] = put(es.at[d], er.at[d], se, d, sib)
    xcp = {}
    for d in eo:
        scp[d].wait_recv()
        v = ot[d, :, c] + er[d].astype(F32)
        ea[d] = v
        ex[d] = v.astype(BF16)
        xcp[d] = [put(ex.at[d, lax.rem(x + e, 4)], exr.at[d, e - 1], se, 3 + 3 * d + e, xp(e)) for e in (2, 1, 3)]
    ycp = []
    for d in eo:
        for cp in xcp[d]:
            cp.wait_recv()
        v = ea[d, x]
        for e in range(3):
            v = v + exr[d, e].astype(F32)
        if d:
            ey[d - 1] = v.astype(BF16)
            ycp.append(put(ey.at[d - 1], eyr.at[d - 1], se, 15 + d, ylp(d)))
    for cp in ycp:
        cp.wait_recv()
    for d in range(3):
        v = v + eyr[d].astype(F32)
    r = (xcols + v).astype(BF16)

    sf = (f_s, f_r)
    cb[z, x, c] = r
    rb[y] = r
    mine = cb.at[z, x, c]
    zcp = {d: put(mine, mine, sf, d, zp(d)) for d in (4, 3, 5, 2, 6, 1, 7)}
    xcp = {0: [put(mine, mine, sf, 7 + e, xp(e)) for e in (2, 1, 3)]}
    ycp = [put(mine, rb.at[y], sf, 10 + d, yp(d)) for d in (4, 3, 5, 2, 6, 1, 7)]
    csum = lax.dot_general(r, onehot, NT, preferred_element_type=F32)
    cross_ref[...] = csum / jnp.maximum(counts[0:1, :], 1.0)
    fo = (0, 1, 7, 2, 6, 3, 5, 4)
    for d in fo[1:]:
        zcp[d].wait_recv()
        blk = cb.at[lax.rem(z + 8 - d, 8), x, c]
        xcp[d] = [put(blk, blk, sf, 17 + 3 * d - 3 + e, xp(e)) for e in (2, 1, 3)]
    scp = {}
    for d in fo:
        for cp in xcp[d]:
            cp.wait_recv()
        blk = cb.at[lax.rem(z + 8 - d, 8), :, c]
        scp[d] = put(blk, blk, sf, 39 + d, sib)
    for cp in ycp:
        cp.wait_recv()
    rows = rb[...].reshape(128, 512)
    gcp = []
    for i, d in enumerate(fo):
        scp[d].wait_recv()
        g = lax.dot_general(rows, cb[lax.rem(z + 8 - d, 8)].reshape(128, 512), NT, preferred_element_type=F32)
        gt[i // 4, :, :, i % 4 * 128:(i % 4 + 1) * 128] = (g * (1.0 / 512.0)).astype(BF16).reshape(8, 16, 128)
        if i % 4 == 3:
            p = i // 4
            gcp += [put(gt.at[p, lax.rem(y + e, 8)], gr.at[p, y], sf, 46 + 7 * p + e, yp(e))
                    for e in (4, 3, 5, 2, 6, 1, 7)]
            gr[p, y] = gt[p, y]
    for cp in gcp:
        cp.wait_recv()
    for i, d in enumerate(fo):
        q = lax.rem(z + 8 - d, 8)
        for yy in range(8):
            o = pl.multiple_of((q * 2 + yy // 4) * 512 + yy % 4 * 128, 128)
            gram_ref[:, pl.ds(o, 128)] = gr[i // 4, yy, :, i % 4 * 128:(i % 4 + 1) * 128].astype(F32)

    for cp in sends:
        cp.wait_send()


def on_device(resid_in, norm_gain, gate_weight, up_weight, down_weight, labels):
    vm = pl.BlockSpec(memory_space=pltpu.VMEM)
    hbm = pl.BlockSpec(memory_space=pltpu.HBM)
    dma = pltpu.SemaphoreType.DMA
    scratch = [
        pltpu.VMEM((4, 4, 2, 16, 512), BF16),
        pltpu.VMEM((512, 512), BF16),
        pltpu.VMEM((512, 896), BF16),
        pltpu.VMEM((512, 896), BF16),
        pltpu.VMEM((896, 512), BF16),
        pltpu.VMEM((512, 896), BF16),
        pltpu.VMEM((8, 128), F32),
        pltpu.VMEM((7, 8, 128), F32),
        pltpu.VMEM((2, 8, 128), F32),
        pltpu.VMEM((8, 4, 16, 1792), F32),
        pltpu.VMEM((4, 2, 4, 16, 1792), BF16),
        pltpu.VMEM((4, 2, 4, 16, 1792), BF16),
        pltpu.VMEM((4, 16, 1792), F32),
        pltpu.VMEM((4, 16, 1792), BF16),
        pltpu.VMEM((4, 16, 1792), BF16),
        pltpu.VMEM((8, 4, 16, 896), BF16),
        pltpu.VMEM((4, 4, 2, 16, 512), F32),
        pltpu.VMEM((4, 4, 16, 512), BF16),
        pltpu.VMEM((4, 4, 16, 512), BF16),
        pltpu.VMEM((4, 4, 16, 512), F32),
        pltpu.VMEM((4, 4, 16, 512), BF16),
        pltpu.VMEM((4, 3, 16, 512), BF16),
        pltpu.VMEM((3, 16, 512), BF16),
        pltpu.VMEM((3, 16, 512), BF16),
        pltpu.VMEM((8, 4, 2, 16, 512), BF16),
        pltpu.VMEM((8, 16, 512), BF16),
        pltpu.VMEM((2, 8, 16, 512), BF16),
        pltpu.VMEM((2, 8, 16, 512), BF16),
        dma((3,)),
        dma((19,)), dma((19,)),
        dma((8,)), dma((8,)),
        dma((4, 2, 4)), dma((4, 2, 4)),
        dma((4,)), dma((4,)),
        dma((4, 2, 4)), dma((4, 2, 4)),
        dma((19,)), dma((19,)),
        dma((61,)), dma((61,)),
    ]
    return pl.pallas_call(
        kernel,
        out_shape=(jax.ShapeDtypeStruct((16, 8192), F32), jax.ShapeDtypeStruct((16, CLASSES), F32)),
        in_specs=[vm, vm, hbm, hbm, hbm, vm],
        out_specs=(vm, vm),
        scratch_shapes=scratch,
        compiler_params=pltpu.CompilerParams(
            collective_id=0, has_side_effects=True, vmem_limit_bytes=60 * 2**20),
    )(resid_in, norm_gain.reshape(1, -1), gate_weight, up_weight, down_weight, labels.reshape(1, -1))


def solution(mesh):
    return jax.shard_map(
        on_device,
        mesh=mesh,
        in_specs=(P("hid", "tok"), P("tok"), P("tok", "hid"), P("tok", "hid"), P("hid", "tok"), P()),
        out_specs=(P(("tok", "hid"), None), P(("tok", "hid"), None)),
        check_vma=False,
    )
```

```python
import jax
import jax.numpy as jnp
from jax import lax
from jax.experimental import pallas as pl
from jax.experimental.pallas import tpu as pltpu
from jax.sharding import PartitionSpec as P

CLASSES = 64
EPS = 1e-05
F32 = jnp.float32
BF16 = jnp.bfloat16
MESH = pl.DeviceIdType.MESH
NT = (((1,), (1,)), ((), ()))


def kernel(x_ref, gain_ref, wg_hbm, wu_hbm, wd_hbm, lab_ref, gram_ref, cross_ref,
           xg, xn, wg, wu, wd, wdt, sqb, sqz, sqp, cown0, cown1, csend0, csend1, crecv0, crecv1,
           fin0, fin1, ysend0, ysend1, yrecv0, yrecv1, hb0, hb1, ot, es, er, ea, ex, exr, ey, eyr, cb, rb, gt, gr,
           wsem, a_s, a_r, q_s, q_r, c_s, c_r, y_s, y_r, d_s, d_r, e_s, e_r, f_s, f_r):
    t = lax.axis_index("tok")
    h = lax.axis_index("hid")
    z, yh = t // 2, lax.rem(t, 2)
    yl, x, c = h // 8, lax.rem(h // 2, 4), lax.rem(h, 2)
    y = yh * 4 + yl

    def at(z=z, y=y, x=x, c=c):
        return {"tok": z * 2 + y // 4, "hid": (lax.rem(y, 4) * 4 + x) * 2 + c}

    def zp(d):
        return at(z=lax.rem(z + d, 8))

    def yp(d):
        return at(y=lax.rem(y + d, 8))

    def ylp(d):
        return at(y=yh * 4 + lax.rem(yl + d, 4))

    def xp(d):
        return at(x=lax.rem(x + d, 4))

    sib = at(c=1 - c)
    part = yp(4)

    loads = [pltpu.make_async_copy(a, b, wsem.at[i])
             for i, (a, b) in enumerate(((wg_hbm, wg), (wu_hbm, wu), (wd_hbm, wd)))]
    for cp in loads:
        cp.start()

    barrier = pltpu.get_barrier_semaphore()
    peers = [yp(d) for d in range(1, 8)] + [xp(d) for d in range(1, 4)] + [sib]
    peers += [zp(d) for d in range(1, 8)]
    for p in peers:
        pl.semaphore_signal(barrier, inc=1, device_id=p, device_id_type=MESH)
    xg[yl, x, c] = x_ref[...]
    pl.semaphore_wait(barrier, len(peers))

    sends = []

    def put(src, dst, sem, i, dev):
        cp = pltpu.make_async_remote_copy(src_ref=src, dst_ref=dst, send_sem=sem[0].at[i], recv_sem=sem[1].at[i],
                                          device_id=dev, device_id_type=MESH)
        cp.start()
        sends.append(cp)
        return cp

    sa = (a_s, a_r)
    ycp = {d: put(xg.at[yl, x, c], xg.at[yl, x, c], sa, d - 1, ylp(d)) for d in (2, 3, 1)}
    xcp = [[put(xg.at[yl, x, c], xg.at[yl, x, c], sa, d + 2, xp(d)) for d in (2, 1, 3)]]
    loads[2].wait()
    wdt[...] = wd[...].T
    for d in (1, 2, 3):
        ycp[d].wait_recv()
        b = lax.rem(yl + 4 - d, 4)
        xcp.append([put(xg.at[b, x, c], xg.at[b, x, c], sa, 3 * d + e + 2, xp(e)) for e in (2, 1, 3)])
    scp = []
    for d in range(4):
        for cp in xcp[d]:
            cp.wait_recv()
        b = lax.rem(yl + 4 - d, 4)
        scp.append(put(xg.at[b, :, c], xg.at[b, :, c], sa, 15 + d, sib))
    loads[0].wait()
    loads[1].wait()
    for cp in scp:
        cp.wait_recv()

    xa = xg[...].reshape(512, 512)
    xf = xa.astype(F32)
    xn[...] = (xf * gain_ref[...]).astype(BF16)

    cown, csend, crecv = (cown0, cown1), (csend0, csend1), (crecv0, crecv1)
    fin, ysend, yrecv, hb = (fin0, fin1), (ysend0, ysend1), (yrecv0, yrecv1), (hb0, hb1)
    width = (512, 384)

    def own(r):
        q = lax.rem(z + r, 8)
        rows = xn[pl.ds(pl.multiple_of(q * 64, 64), 64), :]
        for b in (0, 1):
            n, lo = width[b], 512 * b
            for i, w in ((0, wg), (1, wu)):
                v = jnp.dot(rows, w[:, lo:lo + n], preferred_element_type=F32)
                cown[b][r, :, :, i * n:(i + 1) * n] = v.reshape(2, 32, n)

    right, left = zp(1), zp(7)
    sc = (c_s, c_r)
    ring = {}

    def hop(b, k, way, s, add):
        v = cown[b][4 - k if way == 0 else 4 + k, s]
        if add:
            ring[b, k - 1, way, s].wait_recv()
            v = v + crecv[b][k - 1, way, s].astype(F32)
        csend[b][k, way, s] = v.astype(BF16)
        ring[b, k, way, s] = put(csend[b].at[k, way, s], crecv[b].at[k, way, s], sc, (b, k, way, s),
                                 right if way == 0 else left)

    def first(b):
        hop(b, 0, 0, 0, False)
        hop(b, 0, 1, 1, False)

    def second(b):
        hop(b, 1, 0, 1, False)
        hop(b, 1, 1, 0, False)

    def third(b):
        hop(b, 1, 0, 0, True)
        hop(b, 1, 1, 1, True)

    def later(b, k):
        for way, s in ((0, 1), (1, 0), (0, 0), (1, 1)):
            hop(b, k, way, s, True)

    own(4)
    first(0)
    own(3)
    own(5)
    second(0)
    first(1)

    x2 = xf * xf
    hi = x2.astype(BF16)
    lo = (x2 - hi.astype(F32)).astype(BF16)
    ones = jnp.ones((8, 512), BF16)
    sq = (lax.dot_general(ones, hi, NT, preferred_element_type=F32)
          + lax.dot_general(ones, lo, NT, preferred_element_type=F32))
    sqb[...] = jnp.zeros_like(sqb)
    for k in range(4):
        sqb[k:k + 1, :] = sq[0:1, k * 128:(k + 1) * 128]
    sqs = (q_s, q_r)
    third(0)
    second(1)
    own(2)
    own(6)
    later(0, 2)
    third(1)
    qcps = [put(sqb, sqz.at[d - 1], sqs, d - 1, zp(d)) for d in range(1, 8)]
    own(1)
    own(7)
    later(0, 3)
    later(1, 2)
    own(0)

    sel = (lax.broadcasted_iota(jnp.int32, (16, 512), 1)
           == lax.broadcasted_iota(jnp.int32, (16, 512), 0) + h * 16).astype(BF16)
    xcols = lax.dot_general(sel, xa, NT, preferred_element_type=F32)
    onehot = (lax.broadcasted_iota(jnp.int32, (CLASSES, 512), 0) == lab_ref[...]).astype(BF16)
    counts = lax.dot_general(ones, onehot, NT, preferred_element_type=F32)

    sy = (y_s, y_r)

    def swap(b):
        cps = []
        for s in (0, 1):
            for way in (0, 1):
                ring[b, 3, way, s].wait_recv()
            v = cown[b][0, s] + crecv[b][3, 0, s].astype(F32) + crecv[b][3, 1, s].astype(F32)
            fin[b][s] = v
            ysend[b][s] = v.astype(BF16)
            cps.append(put(ysend[b].at[s], yrecv[b].at[s], sy, (b, s), part))
        return cps

    ycps = [swap(0)]
    later(1, 3)
    for cp in qcps:
        cp.wait_recv()
    tot = sqb[...]
    for d in range(7):
        tot = tot + sqz[d]
    sqp[0] = tot
    qy = put(sqp.at[0], sqp.at[1], sqs, 7, part)
    ycps.append(swap(1))
    qy.wait_recv()
    tot = sqp[0] + sqp[1]
    tix = (lax.broadcasted_iota(jnp.int32, (64, 128), 0) + z * 64
           - lax.broadcasted_iota(jnp.int32, (64, 128), 1))
    pick = jnp.zeros((64, 128), F32)
    for k in range(4):
        pick = pick + jnp.where(tix == k * 128, tot[k:k + 1, :], 0.0)
    scale = lax.rsqrt(jnp.sum(pick, axis=1, keepdims=True) / 8192.0 + EPS)

    sd = (d_s, d_r)
    live = {}

    def dput(b, r, s, j, d):
        blk = hb[b].at[lax.rem(z + r, 8), s]
        live[b, j, s] = put(blk, blk, sd, (b, j, s), zp(d))

    def hidden(b):
        n = width[b]
        for s in (0, 1):
            ycps[b][s].wait_recv()
            v = (fin[b][s] + yrecv[b][s].astype(F32)) * scale[s * 32:(s + 1) * 32, :]
            gate, up = v[:, :n], v[:, n:]
            hb[b][z, s] = (gate / (1.0 + jnp.exp(-gate)) * up).astype(BF16)
            for j, d in enumerate((2, 6, 1, 7)):
                dput(b, 0, s, j, d)

    def onward(b):
        for s in (0, 1):
            live[b, 0, s].wait_recv()
            if s == 0:
                dput(b, 6, s, 6, 2)
            dput(b, 6, s, 4, 1)
            live[b, 1, s].wait_recv()
            if s == 1:
                dput(b, 2, s, 7, 6)
            dput(b, 2, s, 5, 7)

    def arrived(b):
        for s in (0, 1):
            for j in (2, 3, 4, 5, 6 + s):
                live[b, j, s].wait_recv()

    eo = (2, 1, 3, 0)

    def down(b, d):
        rows = wdt[pl.ds(pl.multiple_of(lax.rem(yl + d, 4) * 128, 128), 128), 512 * b:512 * b + width[b]]
        v = lax.dot_general(rows, hb[b][...].reshape(512, width[b]), NT, preferred_element_type=F32)
        return v.reshape(4, 2, 16, 512)

    hidden(0)
    onward(0)
    hidden(1)
    arrived(0)
    onward(1)
    for d in eo:
        ot[d] = down(0, d)
    arrived(1)

    se = (e_s, e_r)
    scp = {}
    for d in eo:
        ot[d] = ot[d] + down(1, d)
        es[d] = ot[d, :, 1 - c].astype(BF16)
        scp[d] = put(es.at[d], er.at[d], se, d, sib)
    xcp = {}
    for d in eo:
        scp[d].wait_recv()
        v = ot[d, :, c] + er[d].astype(F32)
        ea[d] = v
        ex[d] = v.astype(BF16)
        xcp[d] = [put(ex.at[d, lax.rem(x + e, 4)], exr.at[d, e - 1], se, 3 + 3 * d + e, xp(e)) for e in (2, 1, 3)]
    ycp = []
    for d in eo:
        for cp in xcp[d]:
            cp.wait_recv()
        v = ea[d, x]
        for e in range(3):
            v = v + exr[d, e].astype(F32)
        if d:
            ey[d - 1] = v.astype(BF16)
            ycp.append(put(ey.at[d - 1], eyr.at[d - 1], se, 15 + d, ylp(d)))
    for cp in ycp:
        cp.wait_recv()
    for d in range(3):
        v = v + eyr[d].astype(F32)
    r = (xcols + v).astype(BF16)

    sf = (f_s, f_r)
    cb[z, x, c] = r
    rb[y] = r
    mine = cb.at[z, x, c]
    zcp = {d: put(mine, mine, sf, d, zp(d)) for d in (4, 3, 5, 2, 6, 1, 7)}
    xcp = {0: [put(mine, mine, sf, 7 + e, xp(e)) for e in (2, 1, 3)]}
    ycp = [put(mine, rb.at[y], sf, 10 + d, yp(d)) for d in (4, 3, 5, 2, 6, 1, 7)]
    csum = lax.dot_general(r, onehot, NT, preferred_element_type=F32)
    cross_ref[...] = csum / jnp.maximum(counts[0:1, :], 1.0)
    fo = (0, 1, 7, 2, 6, 3, 5, 4)
    for d in fo[1:]:
        zcp[d].wait_recv()
        blk = cb.at[lax.rem(z + 8 - d, 8), x, c]
        xcp[d] = [put(blk, blk, sf, 17 + 3 * d - 3 + e, xp(e)) for e in (2, 1, 3)]
    scp = {}
    for d in fo:
        for cp in xcp[d]:
            cp.wait_recv()
        blk = cb.at[lax.rem(z + 8 - d, 8), :, c]
        scp[d] = put(blk, blk, sf, 39 + d, sib)
    for cp in ycp:
        cp.wait_recv()
    rows = rb[...].reshape(128, 512)
    gcp = []
    for i, d in enumerate(fo):
        scp[d].wait_recv()
        g = lax.dot_general(rows, cb[lax.rem(z + 8 - d, 8)].reshape(128, 512), NT, preferred_element_type=F32)
        gt[i // 4, :, :, i % 4 * 128:(i % 4 + 1) * 128] = (g * (1.0 / 512.0)).astype(BF16).reshape(8, 16, 128)
        if i % 4 == 3:
            p = i // 4
            gcp += [put(gt.at[p, lax.rem(y + e, 8)], gr.at[p, y], sf, 46 + 7 * p + e, yp(e))
                    for e in (4, 3, 5, 2, 6, 1, 7)]
            gr[p, y] = gt[p, y]
    for cp in gcp:
        cp.wait_recv()
    for i, d in enumerate(fo):
        q = lax.rem(z + 8 - d, 8)
        for yy in range(8):
            o = pl.multiple_of((q * 2 + yy // 4) * 512 + yy % 4 * 128, 128)
            gram_ref[:, pl.ds(o, 128)] = gr[i // 4, yy, :, i % 4 * 128:(i % 4 + 1) * 128].astype(F32)

    for cp in sends:
        cp.wait_send()


def on_device(resid_in, norm_gain, gate_weight, up_weight, down_weight, labels):
    vm = pl.BlockSpec(memory_space=pltpu.VMEM)
    hbm = pl.BlockSpec(memory_space=pltpu.HBM)
    dma = pltpu.SemaphoreType.DMA
    scratch = [
        pltpu.VMEM((4, 4, 2, 16, 512), BF16),
        pltpu.VMEM((512, 512), BF16),
        pltpu.VMEM((512, 896), BF16),
        pltpu.VMEM((512, 896), BF16),
        pltpu.VMEM((896, 512), BF16),
        pltpu.VMEM((512, 896), BF16),
        pltpu.VMEM((8, 128), F32),
        pltpu.VMEM((7, 8, 128), F32),
        pltpu.VMEM((2, 8, 128), F32),
        pltpu.VMEM((8, 2, 32, 1024), F32),
        pltpu.VMEM((8, 2, 32, 768), F32),
        pltpu.VMEM((4, 2, 2, 32, 1024), BF16),
        pltpu.VMEM((4, 2, 2, 32, 768), BF16),
        pltpu.VMEM((4, 2, 2, 32, 1024), BF16),
        pltpu.VMEM((4, 2, 2, 32, 768), BF16),
        pltpu.VMEM((2, 32, 1024), F32),
        pltpu.VMEM((2, 32, 768), F32),
        pltpu.VMEM((2, 32, 1024), BF16),
        pltpu.VMEM((2, 32, 768), BF16),
        pltpu.VMEM((2, 32, 1024), BF16),
        pltpu.VMEM((2, 32, 768), BF16),
        pltpu.VMEM((8, 2, 32, 512), BF16),
        pltpu.VMEM((8, 2, 32, 384), BF16),
        pltpu.VMEM((4, 4, 2, 16, 512), F32),
        pltpu.VMEM((4, 4, 16, 512), BF16),
        pltpu.VMEM((4, 4, 16, 512), BF16),
        pltpu.VMEM((4, 4, 16, 512), F32),
        pltpu.VMEM((4, 4, 16, 512), BF16),
        pltpu.VMEM((4, 3, 16, 512), BF16),
        pltpu.VMEM((3, 16, 512), BF16),
        pltpu.VMEM((3, 16, 512), BF16),
        pltpu.VMEM((8, 4, 2, 16, 512), BF16),
        pltpu.VMEM((8, 16, 512), BF16),
        pltpu.VMEM((2, 8, 16, 512), BF16),
        pltpu.VMEM((2, 8, 16, 512), BF16),
        dma((3,)),
        dma((19,)), dma((19,)),
        dma((8,)), dma((8,)),
        dma((2, 4, 2, 2)), dma((2, 4, 2, 2)),
        dma((2, 2)), dma((2, 2)),
        dma((2, 8, 2)), dma((2, 8, 2)),
        dma((19,)), dma((19,)),
        dma((61,)), dma((61,)),
    ]
    return pl.pallas_call(
        kernel,
        out_shape=(jax.ShapeDtypeStruct((16, 8192), F32), jax.ShapeDtypeStruct((16, CLASSES), F32)),
        in_specs=[vm, vm, hbm, hbm, hbm, vm],
        out_specs=(vm, vm),
        scratch_shapes=scratch,
        compiler_params=pltpu.CompilerParams(
            collective_id=0, has_side_effects=True, vmem_limit_bytes=60 * 2**20),
    )(resid_in, norm_gain.reshape(1, -1), gate_weight, up_weight, down_weight, labels.reshape(1, -1))


def solution(mesh):
    return jax.shard_map(
        on_device,
        mesh=mesh,
        in_specs=(P("hid", "tok"), P("tok"), P("tok", "hid"), P("tok", "hid"), P("hid", "tok"), P()),
        out_specs=(P(("tok", "hid"), None), P(("tok", "hid"), None)),
        check_vma=False,
    )
```

```python
import jax
import jax.numpy as jnp
from jax import lax
from jax.experimental import pallas as pl
from jax.experimental.pallas import tpu as pltpu
from jax.sharding import PartitionSpec as P

CLASSES = 64
EPS = 1e-05
F32 = jnp.float32
BF16 = jnp.bfloat16
MESH = pl.DeviceIdType.MESH
NT = (((1,), (1,)), ((), ()))
ARRIVAL = (0, 1, 7, 2, 6, 3, 5, 4)


def kernel(x_ref, gain_ref, wg_hbm, wu_hbm, wd_hbm, lab_ref, out_ref, cross_ref,
           xg, xn, wg, wu, wd, wdt, sqb, sqz, sqp, cown0, cown1, csend0, csend1, crecv0, crecv1,
           fin0, fin1, ysend0, ysend1, yrecv0, yrecv1, hb0, hb1, ot, es, er, ea, ex, exr, ey, eyr, cb, rb, gt, gr,
           wsem, a_s, a_r, q_s, q_r, c_s, c_r, y_s, y_r, d_s, d_r, e_s, e_r, f_s, f_r):
    t = lax.axis_index("tok")
    h = lax.axis_index("hid")
    z, yh = t // 2, lax.rem(t, 2)
    yl, x, c = h // 8, lax.rem(h // 2, 4), lax.rem(h, 2)
    y = yh * 4 + yl

    def at(z=z, y=y, x=x, c=c):
        return {"tok": z * 2 + y // 4, "hid": (lax.rem(y, 4) * 4 + x) * 2 + c}

    def zp(d):
        return at(z=lax.rem(z + d, 8))

    def yp(d):
        return at(y=lax.rem(y + d, 8))

    def ylp(d):
        return at(y=yh * 4 + lax.rem(yl + d, 4))

    def xp(d):
        return at(x=lax.rem(x + d, 4))

    sib = at(c=1 - c)
    part = yp(4)

    loads = [pltpu.make_async_copy(a, b, wsem.at[i])
             for i, (a, b) in enumerate(((wg_hbm, wg), (wu_hbm, wu), (wd_hbm, wd)))]
    for cp in loads:
        cp.start()

    barrier = pltpu.get_barrier_semaphore()
    peers = [yp(d) for d in range(1, 8)] + [xp(d) for d in range(1, 4)] + [sib]
    peers += [zp(d) for d in range(1, 8)]
    for p in peers:
        pl.semaphore_signal(barrier, inc=1, device_id=p, device_id_type=MESH)
    xg[yl, x, c] = x_ref[...]
    pl.semaphore_wait(barrier, len(peers))

    sends = []

    def put(src, dst, sem, i, dev):
        cp = pltpu.make_async_remote_copy(src_ref=src, dst_ref=dst, send_sem=sem[0].at[i], recv_sem=sem[1].at[i],
                                          device_id=dev, device_id_type=MESH)
        cp.start()
        sends.append(cp)
        return cp

    sa = (a_s, a_r)
    ycp = {d: put(xg.at[yl, x, c], xg.at[yl, x, c], sa, d - 1, ylp(d)) for d in (2, 3, 1)}
    xcp = [[put(xg.at[yl, x, c], xg.at[yl, x, c], sa, d + 2, xp(d)) for d in (2, 1, 3)]]
    loads[2].wait()
    wdt[...] = wd[...].T
    for d in (1, 2, 3):
        ycp[d].wait_recv()
        b = lax.rem(yl + 4 - d, 4)
        xcp.append([put(xg.at[b, x, c], xg.at[b, x, c], sa, 3 * d + e + 2, xp(e)) for e in (2, 1, 3)])
    scp = []
    for d in range(4):
        for cp in xcp[d]:
            cp.wait_recv()
        b = lax.rem(yl + 4 - d, 4)
        scp.append(put(xg.at[b, :, c], xg.at[b, :, c], sa, 15 + d, sib))
    loads[0].wait()
    loads[1].wait()
    for cp in scp:
        cp.wait_recv()

    xa = xg[...].reshape(512, 512)
    xf = xa.astype(F32)
    xn[...] = (xf * gain_ref[...]).astype(BF16)

    cown, csend, crecv = (cown0, cown1), (csend0, csend1), (crecv0, crecv1)
    fin, ysend, yrecv, hb = (fin0, fin1), (ysend0, ysend1), (yrecv0, yrecv1), (hb0, hb1)
    width = (384, 512)

    def own(r):
        q = lax.rem(z + r, 8)
        rows = xn[pl.ds(pl.multiple_of(q * 64, 64), 64), :]
        for b in (0, 1):
            n, lo = width[b], width[0] * b
            for i, w in ((0, wg), (1, wu)):
                v = jnp.dot(rows, w[:, lo:lo + n], preferred_element_type=F32)
                cown[b][r, :, :, i * n:(i + 1) * n] = v.reshape(2, 32, n)

    right, left = zp(1), zp(7)
    sc = (c_s, c_r)
    ring = {}

    def hop(b, k, way, s, add):
        v = cown[b][4 - k if way == 0 else 4 + k, s]
        if add:
            ring[b, k - 1, way, s].wait_recv()
            v = v + crecv[b][k - 1, way, s].astype(F32)
        csend[b][k, way, s] = v.astype(BF16)
        ring[b, k, way, s] = put(csend[b].at[k, way, s], crecv[b].at[k, way, s], sc, (b, k, way, s),
                                 right if way == 0 else left)

    def first(b):
        hop(b, 0, 0, 0, False)
        hop(b, 0, 1, 1, False)

    def second(b):
        hop(b, 1, 0, 1, False)
        hop(b, 1, 1, 0, False)

    def third(b):
        hop(b, 1, 0, 0, True)
        hop(b, 1, 1, 1, True)

    def later(b, k):
        for way, s in ((0, 1), (1, 0), (0, 0), (1, 1)):
            hop(b, k, way, s, True)

    own(4)
    first(0)
    own(3)
    own(5)
    second(0)
    first(1)

    x2 = xf * xf
    hi = x2.astype(BF16)
    lo = (x2 - hi.astype(F32)).astype(BF16)
    ones = jnp.ones((8, 512), BF16)
    sq = (lax.dot_general(ones, hi, NT, preferred_element_type=F32)
          + lax.dot_general(ones, lo, NT, preferred_element_type=F32))
    sqb[...] = jnp.zeros_like(sqb)
    for k in range(4):
        sqb[k:k + 1, :] = sq[0:1, k * 128:(k + 1) * 128]
    sqs = (q_s, q_r)
    third(0)
    second(1)
    own(2)
    own(6)
    later(0, 2)
    third(1)
    qcps = [put(sqb, sqz.at[d - 1], sqs, d - 1, zp(d)) for d in range(1, 8)]
    own(1)
    own(7)
    later(0, 3)
    later(1, 2)
    own(0)

    sel = (lax.broadcasted_iota(jnp.int32, (16, 512), 1)
           == lax.broadcasted_iota(jnp.int32, (16, 512), 0) + h * 16).astype(BF16)
    xcols = lax.dot_general(sel, xa, NT, preferred_element_type=F32)
    onehot = (lax.broadcasted_iota(jnp.int32, (CLASSES, 512), 0) == lab_ref[...]).astype(BF16)
    counts = lax.dot_general(ones, onehot, NT, preferred_element_type=F32)

    sy = (y_s, y_r)

    def swap(b):
        cps = []
        for s in (0, 1):
            for way in (0, 1):
                ring[b, 3, way, s].wait_recv()
            v = cown[b][0, s] + crecv[b][3, 0, s].astype(F32) + crecv[b][3, 1, s].astype(F32)
            fin[b][s] = v
            ysend[b][s] = v.astype(BF16)
            cps.append(put(ysend[b].at[s], yrecv[b].at[s], sy, (b, s), part))
        return cps

    ycps = [swap(0)]
    later(1, 3)
    for cp in qcps:
        cp.wait_recv()
    tot = sqb[...]
    for d in range(7):
        tot = tot + sqz[d]
    sqp[0] = tot
    qy = put(sqp.at[0], sqp.at[1], sqs, 7, part)
    ycps.append(swap(1))
    qy.wait_recv()
    tot = sqp[0] + sqp[1]
    tix = (lax.broadcasted_iota(jnp.int32, (64, 128), 0) + z * 64
           - lax.broadcasted_iota(jnp.int32, (64, 128), 1))
    pick = jnp.zeros((64, 128), F32)
    for k in range(4):
        pick = pick + jnp.where(tix == k * 128, tot[k:k + 1, :], 0.0)
    scale = lax.rsqrt(jnp.sum(pick, axis=1, keepdims=True) / 8192.0 + EPS)

    sd = (d_s, d_r)
    live = {}

    def dput(b, r, s, j, d):
        blk = hb[b].at[lax.rem(z + r, 8), s]
        live[b, j, s] = put(blk, blk, sd, (b, j, s), zp(d))

    def hidden(b):
        n = width[b]
        for s in (0, 1):
            ycps[b][s].wait_recv()
            v = (fin[b][s] + yrecv[b][s].astype(F32)) * scale[s * 32:(s + 1) * 32, :]
            gate, up = v[:, :n], v[:, n:]
            hb[b][z, s] = (gate / (1.0 + jnp.exp(-gate)) * up).astype(BF16)
            for j, d in enumerate((2, 6, 1, 7)):
                dput(b, 0, s, j, d)

    def onward(b):
        for s in (0, 1):
            live[b, 0, s].wait_recv()
            if s == 0:
                dput(b, 6, s, 6, 2)
            dput(b, 6, s, 4, 1)
            live[b, 1, s].wait_recv()
            if s == 1:
                dput(b, 2, s, 7, 6)
            dput(b, 2, s, 5, 7)

    def arrived(b):
        for s in (0, 1):
            for j in (2, 3, 4, 5, 6 + s):
                live[b, j, s].wait_recv()

    eo = (2, 1, 3, 0)

    def down(b, d):
        rows = wdt[pl.ds(pl.multiple_of(lax.rem(yl + d, 4) * 128, 128), 128), width[0] * b:width[0] * b + width[b]]
        v = lax.dot_general(rows, hb[b][...].reshape(512, width[b]), NT, preferred_element_type=F32)
        return v.reshape(4, 2, 16, 512)

    hidden(0)
    onward(0)
    hidden(1)
    arrived(0)
    onward(1)
    for d in eo:
        ot[d] = down(0, d)
    arrived(1)

    se = (e_s, e_r)
    scp = {}
    for d in eo:
        ot[d] = ot[d] + down(1, d)
        es[d] = ot[d, :, 1 - c].astype(BF16)
        scp[d] = put(es.at[d], er.at[d], se, d, sib)
    xcp = {}
    for d in eo:
        scp[d].wait_recv()
        v = ot[d, :, c] + er[d].astype(F32)
        ea[d] = v
        ex[d] = v.astype(BF16)
        xcp[d] = [put(ex.at[d, lax.rem(x + e, 4)], exr.at[d, e - 1], se, 3 + 3 * d + e, xp(e)) for e in (2, 1, 3)]
    ycp = []
    for d in eo:
        for cp in xcp[d]:
            cp.wait_recv()
        v = ea[d, x]
        for e in range(3):
            v = v + exr[d, e].astype(F32)
        if d:
            ey[d - 1] = v.astype(BF16)
            ycp.append(put(ey.at[d - 1], eyr.at[d - 1], se, 15 + d, ylp(d)))
    for cp in ycp:
        cp.wait_recv()
    for d in range(3):
        v = v + eyr[d].astype(F32)
    r = (xcols + v).astype(BF16)

    sf = (f_s, f_r)
    cb[z, x, c] = r
    rb[y] = r
    mine = cb.at[z, x, c]
    zcp = {d: put(mine, mine, sf, d, zp(d)) for d in (4, 3, 5, 2, 6, 1, 7)}
    xcp = {0: [put(mine, mine, sf, 7 + e, xp(e)) for e in (2, 1, 3)]}
    ycp = [put(mine, rb.at[y], sf, 10 + d, yp(d)) for d in (4, 3, 5, 2, 6, 1, 7)]
    csum = lax.dot_general(r, onehot, NT, preferred_element_type=F32)
    cross_ref[...] = csum / jnp.maximum(counts[0:1, :], 1.0)
    fo = ARRIVAL
    for d in fo[1:]:
        zcp[d].wait_recv()
        blk = cb.at[lax.rem(z + 8 - d, 8), x, c]
        xcp[d] = [put(blk, blk, sf, 17 + 3 * d - 3 + e, xp(e)) for e in (2, 1, 3)]
    scp = {}
    for d in fo:
        for cp in xcp[d]:
            cp.wait_recv()
        blk = cb.at[lax.rem(z + 8 - d, 8), :, c]
        scp[d] = put(blk, blk, sf, 39 + d, sib)
    for cp in ycp:
        cp.wait_recv()
    rows = rb[...].reshape(128, 512)
    gcp = []
    for i, d in enumerate(fo):
        scp[d].wait_recv()
        g = lax.dot_general(rows, cb[lax.rem(z + 8 - d, 8)].reshape(128, 512), NT, preferred_element_type=F32)
        gt[i // 4, :, :, i % 4 * 128:(i % 4 + 1) * 128] = (g * (1.0 / 512.0)).astype(BF16).reshape(8, 16, 128)
        if i % 4 == 3:
            p = i // 4
            gcp += [put(gt.at[p, lax.rem(y + e, 8)], gr.at[p, y], sf, 46 + 7 * p + e, yp(e))
                    for e in (4, 3, 5, 2, 6, 1, 7)]
            gr[p, y] = gt[p, y]
    for cp in gcp:
        cp.wait_recv()
    out_ref[...] = gr[...]

    for cp in sends:
        cp.wait_send()


def place(gr_ref, c_ref, gram_ref, cross_ref):
    z = lax.axis_index("tok") // 2
    for i, d in enumerate(ARRIVAL):
        q = lax.rem(z + 8 - d, 8)
        for yy in range(8):
            o = pl.multiple_of((q * 2 + yy // 4) * 512 + yy % 4 * 128, 128)
            gram_ref[:, pl.ds(o, 128)] = gr_ref[i // 4, yy, :, i % 4 * 128:(i % 4 + 1) * 128].astype(F32)
    cross_ref[...] = c_ref[...]


def on_device(resid_in, norm_gain, gate_weight, up_weight, down_weight, labels):
    vm = pl.BlockSpec(memory_space=pltpu.VMEM)
    hbm = pl.BlockSpec(memory_space=pltpu.HBM)
    dma = pltpu.SemaphoreType.DMA
    scratch = [
        pltpu.VMEM((4, 4, 2, 16, 512), BF16),
        pltpu.VMEM((512, 512), BF16),
        pltpu.VMEM((512, 896), BF16),
        pltpu.VMEM((512, 896), BF16),
        pltpu.VMEM((896, 512), BF16),
        pltpu.VMEM((512, 896), BF16),
        pltpu.VMEM((8, 128), F32),
        pltpu.VMEM((7, 8, 128), F32),
        pltpu.VMEM((2, 8, 128), F32),
        pltpu.VMEM((8, 2, 32, 768), F32),
        pltpu.VMEM((8, 2, 32, 1024), F32),
        pltpu.VMEM((4, 2, 2, 32, 768), BF16),
        pltpu.VMEM((4, 2, 2, 32, 1024), BF16),
        pltpu.VMEM((4, 2, 2, 32, 768), BF16),
        pltpu.VMEM((4, 2, 2, 32, 1024), BF16),
        pltpu.VMEM((2, 32, 768), F32),
        pltpu.VMEM((2, 32, 1024), F32),
        pltpu.VMEM((2, 32, 768), BF16),
        pltpu.VMEM((2, 32, 1024), BF16),
        pltpu.VMEM((2, 32, 768), BF16),
        pltpu.VMEM((2, 32, 1024), BF16),
        pltpu.VMEM((8, 2, 32, 384), BF16),
        pltpu.VMEM((8, 2, 32, 512), BF16),
        pltpu.VMEM((4, 4, 2, 16, 512), F32),
        pltpu.VMEM((4, 4, 16, 512), BF16),
        pltpu.VMEM((4, 4, 16, 512), BF16),
        pltpu.VMEM((4, 4, 16, 512), F32),
        pltpu.VMEM((4, 4, 16, 512), BF16),
        pltpu.VMEM((4, 3, 16, 512), BF16),
        pltpu.VMEM((3, 16, 512), BF16),
        pltpu.VMEM((3, 16, 512), BF16),
        pltpu.VMEM((8, 4, 2, 16, 512), BF16),
        pltpu.VMEM((8, 16, 512), BF16),
        pltpu.VMEM((2, 8, 16, 512), BF16),
        pltpu.VMEM((2, 8, 16, 512), BF16),
        dma((3,)),
        dma((19,)), dma((19,)),
        dma((8,)), dma((8,)),
        dma((2, 4, 2, 2)), dma((2, 4, 2, 2)),
        dma((2, 2)), dma((2, 2)),
        dma((2, 8, 2)), dma((2, 8, 2)),
        dma((19,)), dma((19,)),
        dma((61,)), dma((61,)),
    ]
    pieces, cross = pl.pallas_call(
        kernel,
        out_shape=(jax.ShapeDtypeStruct((2, 8, 16, 512), BF16), jax.ShapeDtypeStruct((16, CLASSES), F32)),
        in_specs=[vm, vm, hbm, hbm, hbm, vm],
        out_specs=(vm, vm),
        scratch_shapes=scratch,
        compiler_params=pltpu.CompilerParams(
            collective_id=0, has_side_effects=True, vmem_limit_bytes=60 * 2**20),
    )(resid_in, norm_gain.reshape(1, -1), gate_weight, up_weight, down_weight, labels.reshape(1, -1))
    return pl.pallas_call(
        place,
        out_shape=(jax.ShapeDtypeStruct((16, 8192), F32), jax.ShapeDtypeStruct((16, CLASSES), F32)),
        in_specs=[vm, vm],
        out_specs=(vm, vm),
    )(pieces, cross)


def solution(mesh):
    return jax.shard_map(
        on_device,
        mesh=mesh,
        in_specs=(P("hid", "tok"), P("tok"), P("tok", "hid"), P("tok", "hid"), P("hid", "tok"), P()),
        out_specs=(P(("tok", "hid"), None), P(("tok", "hid"), None)),
        check_vma=False,
    )
```
